256 devices in a mesh: row: 16 (over x_hi, z), col: 16 (over x_lo, y, core).
Axes of the slice: x: 4 (x_hi: 2, x_lo: 2; x = x_hi * 2 + x_lo), y: 4, z: 8, core: 2. Of those that a mesh axis runs over, the one named last changes fastest.
Arguments:
- tokens: bfloat16 [6016, 8192], P('row', 'col'), may hold values from -6 to 6
- weight: bfloat16 [8192, 26624], P('row', 'col'), may hold values from -0.0625 to 0.0625
Outputs:
- activated: bfloat16 [6016, 26624], P('row', 'col')
The draws below stay inside these ranges and needn't reach their ends.
All inputs are finite; a program needn't handle non-finite values.
Results may differ from the reference program's by a relative error of at most 0.001.
Values may be sent and summed in bfloat16 or wider, within the bound.
No kernel may reach another device: no remote copies, remote signals or barrier semaphores. Data moves between devices by JAX's collectives and lax.ppermute only.
A program may use at most 128 MiB of HBM per device.

```python
import jax
import jax.numpy as jnp

D = 8192
FF = 26624
TOKENS = 6016


def block_scale(rng, shape, shards, least, high):
    factor_of = 1.0
    for axis_at, blocks in shards:
        draws = jax.random.uniform(jax.random.fold_in(jax.random.fold_in(rng, 6), axis_at), (blocks,), jnp.float32, least / len(shards), high / len(shards))
        factor_of = factor_of * jnp.repeat(jnp.exp(draws), shape[axis_at] // blocks).reshape((-1,) + (1,) * (len(shape) - 1 - axis_at))
    return factor_of


def centred(key, dims, width, limit, pieces=(), kind=jnp.bfloat16):
    result = width * jax.random.normal(key, dims, jnp.float32)
    if pieces:
        result = result * block_scale(key, dims, pieces, -0.22, 0.18)
    return jnp.clip(result, -limit, limit).astype(kind)


def setup_inputs(seed: int = 0) -> dict:
    keys = jax.random.split(jax.random.key(seed), 3)
    tokens = centred(keys[0], (TOKENS, D), 1.0, 6.0, ((0, 16), (1, 16)))
    weight = centred(keys[1], (D, FF), D ** -0.5, 0.0625, ((0, 16), (1, 16)))
    return {"tokens": tokens, "weight": weight}


def reference(tokens, weight):
    preact = jnp.dot(tokens, weight, preferred_element_type=jnp.float32)
    return jax.nn.silu(preact).astype(jnp.bfloat16)
```

```python
import jax
import jax.numpy as jnp
from jax import lax
from jax.sharding import Mesh, PartitionSpec as P

AXES = ("xh", "z", "xl", "y", "core")
SIZES = (2, 8, 2, 4, 2)
WIDTHS = (256, 640, 512, 256)


def exchange(value, axis, flip, size):
    return lax.ppermute(value, axis, [(i, i ^ flip) for i in range(size)])


def swap_if(flag, first, second):
    return jnp.where(flag, second, first), jnp.where(flag, first, second)


def gather_tokens(tokens):
    xh, xl, y, core = (lax.axis_index(name) for name in ("xh", "xl", "y", "core"))
    rows, features = tokens.shape
    half = features // 2
    mine, other = swap_if(core == 1, tokens[:, :half], tokens[:, half:])
    received = exchange(other, "core", 1, 2)
    block = jnp.concatenate(swap_if(core == 1, mine, received), axis=1)
    here = block
    beside = exchange(block, ("xh", "xl"), 1, 4)
    across = exchange(block, ("xh", "xl"), 2, 4)
    corner = exchange(block, ("xh", "xl"), 3, 4)
    flip_l = xl != core
    low = swap_if(flip_l, here, beside)
    high = swap_if(flip_l, across, corner)
    flip_h = xh != core
    firsts = swap_if(flip_h, low[0], high[0])
    seconds = swap_if(flip_h, low[1], high[1])
    pieces = []
    for first, second in zip(firsts, seconds):
        pieces.append(
            jnp.concatenate(
                [first[:, :half], second[:, :half], first[:, half:], second[:, half:]], axis=1
            )
        )
    piece = jnp.concatenate(pieces, axis=0)
    width = piece.shape[1]
    out = [jnp.zeros((rows, 4 * width), tokens.dtype) for _ in range(2)]
    for d in range(4):
        arrived = piece if d == 0 else exchange(piece, "y", d, 4)
        for e in range(2):
            out[e] = lax.dynamic_update_slice(
                out[e], arrived[e * rows : (e + 1) * rows], (0, (y ^ d) * width)
            )
    return out


TURN = [(h * 2 + c, c * 2 + h) for h in range(2) for c in range(2)]
CROSS = [(h * 2 + c, c * 2 + 1 - h) for h in range(2) for c in range(2)]


def on_device(tokens, weight):
    xh = lax.axis_index("xh")
    half = weight.shape[0] // 2
    keep, give = gather_tokens(tokens)
    at = 0
    mines = []
    for width in WIDTHS:
        part = weight[:, at : at + width]
        at += width
        if mines:
            part, mines[-1] = lax.optimization_barrier((part, mines[-1]))
        first, second = swap_if(xh == 1, part[:half], part[half:])
        mines.append(
            jnp.concatenate(
                [
                    lax.ppermute(first, ("xh", "core"), TURN),
                    lax.ppermute(second, ("xh", "core"), CROSS),
                ]
            )
        )
    outs = []
    out = None
    for mine in mines:
        whole = lax.all_gather(mine, "z", axis=0, tiled=True)
        if out is not None:
            whole, out = lax.optimization_barrier((whole, out))
            outs.append(lax.ppermute(out, ("xh", "core"), TURN))
        given = jnp.dot(give, whole, preferred_element_type=jnp.float32)
        kept = jnp.dot(keep, whole, preferred_element_type=jnp.float32)
        total = kept + exchange(given, "core", 1, 2)
        out = jax.nn.silu(total).astype(jnp.bfloat16)
    outs.append(lax.ppermute(out, ("xh", "core"), TURN))
    return jnp.concatenate(outs, axis=1)


def solution(mesh):
    fine = Mesh(mesh.devices.reshape(SIZES), AXES)
    placed = P(("xh", "z"), ("xl", "y", "core"))
    return jax.shard_map(
        on_device, mesh=fine, in_specs=(placed, placed), out_specs=placed, check_vma=False
    )
```

```python
import jax
import jax.numpy as jnp
from jax import lax
from jax.sharding import Mesh, PartitionSpec as P

AXES = ("xh", "z", "xl", "y", "core")
SIZES = (2, 8, 2, 4, 2)
WIDTHS = (512, 512, 384, 256)


def exchange(value, axis, flip, size):
    return lax.ppermute(value, axis, [(i, i ^ flip) for i in range(size)])


def swap_if(flag, first, second):
    return jnp.where(flag, second, first), jnp.where(flag, first, second)


def gather_tokens(tokens):
    xh, z, xl, y, core = (lax.axis_index(name) for name in AXES)
    rows, features = tokens.shape
    half = features // 2
    mine, other = swap_if(core == 1, tokens[:, :half], tokens[:, half:])
    received = exchange(other, "core", 1, 2)
    block = jnp.concatenate(swap_if(core == 1, mine, received), axis=1)
    here = block
    beside = exchange(block, ("xh", "xl"), 1, 4)
    across = exchange(block, ("xh", "xl"), 2, 4)
    corner = exchange(block, ("xh", "xl"), 3, 4)
    flip_l = xl != core
    low = swap_if(flip_l, here, beside)
    high = swap_if(flip_l, across, corner)
    flip_h = xh != core
    firsts = swap_if(flip_h, low[0], high[0])
    seconds = swap_if(flip_h, low[1], high[1])
    pieces = []
    for first, second in zip(firsts, seconds):
        pieces.append(
            jnp.concatenate(
                [first[:, :half], second[:, :half], first[:, half:], second[:, half:]], axis=1
            )
        )
    piece = jnp.concatenate(pieces, axis=0)
    out = jnp.zeros((2 * rows, 8 * features), tokens.dtype)
    for d in range(4):
        arrived = piece if d == 0 else exchange(piece, "y", d, 4)
        for c in range(2):
            step = (z - (2 * (y ^ d) + c)) % 8
            out = lax.dynamic_update_slice(
                out, arrived[:, c * features : (c + 1) * features], (0, step * features)
            )
    return out


TURN = [(h * 2 + c, c * 2 + h) for h in range(2) for c in range(2)]
CROSS = [(h * 2 + c, c * 2 + 1 - h) for h in range(2) for c in range(2)]


def along_z(value, shift):
    return lax.ppermute(value, "z", [(i, (i + shift) % 8) for i in range(8)])


def ring(mine):
    half = mine.shape[0] // 2
    arrived = [(0, mine)]
    up = down = mine
    for step in range(1, 4):
        up, down = along_z(up, 1), along_z(down, -1)
        arrived += [(2 * step, up), (2 * (8 - step), down)]
    arrived += [(8, along_z(up[:half], 1)), (9, along_z(down[half:], -1))]
    return arrived


def on_device(tokens, weight):
    xh = lax.axis_index("xh")
    rows = tokens.shape[0]
    half = weight.shape[0] // 2
    at = 0
    rings = []
    for width in WIDTHS:
        part = weight[:, at : at + width]
        at += width
        first, second = swap_if(xh == 1, part[:half], part[half:])
        mine = jnp.concatenate(
            [lax.ppermute(first, ("xh", "core"), TURN), lax.ppermute(second, ("xh", "core"), CROSS)]
        )
        rings.append(ring(mine))
    gathered = gather_tokens(tokens)
    outs = []
    for arrived in rings:
        total = 0
        for block, piece in arrived:
            features = gathered[:, block * half : block * half + piece.shape[0]]
            total += jnp.dot(features, piece, preferred_element_type=jnp.float32)
        total = total[:rows] + exchange(total[rows:], "core", 1, 2)
        out = jax.nn.silu(total).astype(jnp.bfloat16)
        outs.append(lax.ppermute(out, ("xh", "core"), TURN))
    return jnp.concatenate(outs, axis=1)


def solution(mesh):
    fine = Mesh(mesh.devices.reshape(SIZES), AXES)
    placed = P(("xh", "z"), ("xl", "y", "core"))
    return jax.shard_map(
        on_device, mesh=fine, in_specs=(placed, placed), out_specs=placed, check_vma=False
    )
```

```python
import jax
import jax.numpy as jnp
from jax import lax
from jax.experimental import pallas as pl
from jax.experimental.pallas import tpu as pltpu
from jax.sharding import Mesh, PartitionSpec as P

AXES = ("xh", "z", "xl", "y", "core")
SIZES = (2, 8, 2, 4, 2)
WIDTHS = (384, 512, 512, 256)


def exchange(value, axis, flip, size):
    return lax.ppermute(value, axis, [(i, i ^ flip) for i in range(size)])


def swap_if(flag, first, second):
    return jnp.where(flag, second, first), jnp.where(flag, first, second)


def copy_block(rows, columns, source, target):
    target[...] = source[...]


def gather_tokens(tokens):
    z, core = lax.axis_index("z"), lax.axis_index("core")
    rows, features = tokens.shape
    half = features // 2
    mine, other = swap_if(core == 1, tokens[:, :half], tokens[:, half:])
    received = exchange(other, "core", 1, 2)
    block = jnp.concatenate(swap_if(core == 1, mine, received), axis=1)
    plane = lax.all_gather(block, ("xh", "xl", "y"), axis=0, tiled=True)
    at = (z - jnp.arange(8)) % 8
    e, b = jnp.arange(2)[:, None, None], jnp.arange(2)[None, :, None]
    sources = ((core ^ e) * 2 + (core ^ b)) * 4 + at // 2
    sources = jnp.broadcast_to(sources, (2, 2, 8)).reshape(-1).astype(jnp.int32)
    columns = (at % 2).astype(jnp.int32)
    return pl.pallas_call(
        copy_block,
        grid_spec=pltpu.PrefetchScalarGridSpec(
            num_scalar_prefetch=2,
            grid=(2, 2, 8),
            in_specs=[
                pl.BlockSpec(
                    (rows, half), lambda e, b, r, src, col: (src[e * 16 + b * 8 + r], col[r])
                )
            ],
            out_specs=pl.BlockSpec((rows, half), lambda e, b, r, src, col: (e, 2 * r + b)),
        ),
        out_shape=jax.ShapeDtypeStruct((2 * rows, 8 * features), tokens.dtype),
        cost_estimate=pl.CostEstimate(
            flops=0, transcendentals=0, bytes_accessed=4 * 16 * rows * features
        ),
    )(sources, columns, plane)


TURN = [(h * 2 + c, c * 2 + h) for h in range(2) for c in range(2)]
CROSS = [(h * 2 + c, c * 2 + 1 - h) for h in range(2) for c in range(2)]


def along_z(value, shift):
    return lax.ppermute(value, "z", [(i, (i + shift) % 8) for i in range(8)])


def together(*values):
    return lax.optimization_barrier(values)


def step_along_z(step, up, down):
    if step == 4:
        half = up.shape[0] // 2
        up, down = up[:half], down[half:]
    return along_z(up, 1), along_z(down, -1)


def product(gathered, blocks, half):
    total = 0
    for block, piece in blocks:
        features = gathered[:, block * half : block * half + piece.shape[0]]
        total += jnp.dot(features, piece, preferred_element_type=jnp.float32)
    return total


def swapped(part):
    xh = lax.axis_index("xh")
    half = part.shape[0] // 2
    first, second = swap_if(xh == 1, part[:half], part[half:])
    return jnp.concatenate(
        [lax.ppermute(first, ("xh", "core"), TURN), lax.ppermute(second, ("xh", "core"), CROSS)]
    )


def activate(total, rows):
    total = total[:rows] + exchange(total[rows:], "core", 1, 2)
    return jax.nn.silu(total).astype(jnp.bfloat16)


def on_device(tokens, weight):
    rows = tokens.shape[0]
    half = weight.shape[0] // 2
    ends = [sum(WIDTHS[: i + 1]) for i in range(4)]
    parts = [weight[:, end - width : end] for end, width in zip(ends, WIDTHS)]
    gathered = gather_tokens(tokens)
    mine = [None] * 4
    front = [None] * 4
    blocks = [None] * 4
    outs = [None] * 4

    def advance(chunk, step):
        up, down = step_along_z(step, *front[chunk])
        up, down = together(up, down)
        front[chunk] = (up, down)
        if step == 4:
            blocks[chunk] += [(8, up), (9, down)]
        else:
            blocks[chunk] += [(2 * step, up), (2 * (8 - step), down)]

    def begin(chunk, value):
        front[chunk] = (value, value)
        blocks[chunk] = [(0, value)]

    begin(0, swapped(parts[0]))
    parts[1], value = together(parts[1], front[0][0])
    begin(0, value)
    begin(1, swapped(parts[1]))
    for step in range(1, 5):
        advance(0, step)
        if step == 1:
            front[0] = together(*front[0], parts[2])
            *front[0], parts[2] = front[0]
            mine[2] = swapped(parts[2])
        advance(1, step)
        if step == 1:
            *front[1], parts[3] = together(*front[1], parts[3])
            mine[3] = swapped(parts[3])
    for chunk in (2, 3):
        up, down, mine[chunk] = together(*front[chunk - 2], mine[chunk])
        blocks[chunk - 2][-2:] = [(8, up), (9, down)]
        begin(chunk, mine[chunk])
    totals = [product(gathered, blocks[chunk], half) for chunk in (0, 1)]
    for step in range(1, 5):
        for chunk in (2, 3):
            if step == 3:
                *front[chunk], totals[chunk - 2] = together(*front[chunk], totals[chunk - 2])
                outs[chunk - 2] = activate(totals[chunk - 2], rows)
            if step == 4:
                *front[chunk], outs[chunk - 2] = together(*front[chunk], outs[chunk - 2])
            advance(chunk, step)
    outs[2] = activate(product(gathered, blocks[2], half), rows)
    outs[3] = activate(product(gathered, blocks[3], half), rows)
    return jnp.concatenate([lax.ppermute(out, ("xh", "core"), TURN) for out in outs], axis=1)


def solution(mesh):
    fine = Mesh(mesh.devices.reshape(SIZES), AXES)
    placed = P(("xh", "z"), ("xl", "y", "core"))
    return jax.shard_map(
        on_device, mesh=fine, in_specs=(placed, placed), out_specs=placed, check_vma=False
    )
```

```python
import jax
import jax.numpy as jnp
from jax import lax
from jax.sharding import Mesh, PartitionSpec as P

AXES = ("xh", "z", "xl", "y", "core")
SIZES = (2, 8, 2, 4, 2)
WIDTHS = (896, 768)

TURN = [(h * 2 + c, c * 2 + h) for h in range(2) for c in range(2)]
CROSS = [(h * 2 + c, c * 2 + 1 - h) for h in range(2) for c in range(2)]
HOME = [(h * 2 + c, (h ^ c) * 2 + h) for h in range(2) for c in range(2)]


def exchange(value, axis, flip, size):
    return lax.ppermute(value, axis, [(i, i ^ flip) for i in range(size)])


def swap_if(flag, first, second):
    return jnp.where(flag, second, first), jnp.where(flag, first, second)


def together(*values):
    return lax.optimization_barrier(values)


def gather_tokens(tokens):
    z, y, core = (lax.axis_index(name) for name in ("z", "y", "core"))
    rows, features = tokens.shape
    half = features // 2
    mine, other = swap_if(core == 1, tokens[:, :half], tokens[:, half:])
    received = exchange(other, "core", 1, 2)
    near = swap_if(core == 1, mine, received)
    pair = jnp.concatenate(near, axis=1)
    far = exchange(pair, "xl", 1, 2)
    piece = jnp.concatenate([near[0], far[:, :half], near[1], far[:, half:]], axis=1)
    piece = jnp.concatenate([piece, exchange(piece, "xh", 1, 2)], axis=0)
    out = jnp.zeros((2 * rows, 8 * features), tokens.dtype)
    for d in range(4):
        arrived = piece if d == 0 else exchange(piece, "y", d, 4)
        for c in range(2):
            block = (z - (2 * (y ^ d) + c)) % 8
            out = lax.dynamic_update_slice(
                out, arrived[:, c * features : (c + 1) * features], (0, block * features)
            )
    return out


def along_z(value, shift):
    return lax.ppermute(value, "z", [(i, (i + shift) % 8) for i in range(8)])


def step_along_z(step, up, down):
    if step == 4:
        half = up.shape[0] // 2
        up, down = up[:half], down[half:]
    return along_z(up, 1), along_z(down, -1)


def product(gathered, blocks, half):
    total = 0
    for block, piece in blocks:
        features = gathered[:, block * half : block * half + piece.shape[0]]
        total += jnp.dot(features, piece, preferred_element_type=jnp.float32)
    return total


def swapped(part):
    xh, xl, core = (lax.axis_index(name) for name in ("xh", "xl", "core"))
    half = part.shape[0] // 2
    first, second = swap_if(xh == 1, part[:half], part[half:])
    turned = lax.ppermute(first, ("xh", "core"), TURN)
    crossed = lax.ppermute(second, ("xh", "core"), CROSS)
    return jnp.concatenate(swap_if(xl != core, turned, crossed))


def activate(total):
    rows = total.shape[0] // 2
    core = lax.axis_index("core")
    kept, given = swap_if(core == 1, total[:rows], total[rows:])
    total = kept + exchange(given, "core", 1, 2)
    return lax.ppermute(jax.nn.silu(total).astype(jnp.bfloat16), ("xh", "core"), HOME)


def on_device(tokens, weight):
    half = weight.shape[0] // 2
    parts = [weight[:, : WIDTHS[0]], weight[:, WIDTHS[0] :]]
    gathered = gather_tokens(tokens)
    mine = swapped(parts[0])
    mine, parts[1] = together(mine, parts[1])
    mine = [mine, swapped(parts[1])]
    front = [(value, value) for value in mine]
    blocks = [[(0, value)] for value in mine]
    totals = [None, None]
    for step in range(1, 5):
        for chunk in range(2):
            if step == 4:
                totals[chunk] = product(gathered, blocks[chunk][:5], half)
                *front[chunk], totals[chunk] = together(*front[chunk], totals[chunk])
            up, down = together(*step_along_z(step, *front[chunk]))
            front[chunk] = (up, down)
            if step == 4:
                blocks[chunk] += [(8, up), (9, down)]
            else:
                blocks[chunk] += [(2 * step, up), (2 * (8 - step), down)]
    outs = [
        activate(totals[chunk] + product(gathered, blocks[chunk][5:], half)) for chunk in range(2)
    ]
    return jnp.concatenate(outs, axis=1)


def solution(mesh):
    fine = Mesh(mesh.devices.reshape(SIZES), AXES)
    placed = P(("xh", "z"), ("xl", "y", "core"))
    return jax.shard_map(
        on_device, mesh=fine, in_specs=(placed, placed), out_specs=placed, check_vma=False
    )
```

```python
import jax
import jax.numpy as jnp
from jax import lax
from jax.experimental import pallas as pl
from jax.experimental.pallas import tpu as pltpu
from jax.sharding import Mesh, PartitionSpec as P

AXES = ("xh", "z", "xl", "y", "core")
SIZES = (2, 8, 2, 4, 2)
WIDTHS = (384, 512, 512, 256)

TURN = [(h * 2 + c, c * 2 + h) for h in range(2) for c in range(2)]
CROSS = [(h * 2 + c, c * 2 + 1 - h) for h in range(2) for c in range(2)]
HOME = [(h * 2 + c, (h ^ c) * 2 + h) for h in range(2) for c in range(2)]


def exchange(value, axis, flip, size):
    return lax.ppermute(value, axis, [(i, i ^ flip) for i in range(size)])


def swap_if(flag, first, second):
    return jnp.where(flag, second, first), jnp.where(flag, first, second)


def together(*values):
    return lax.optimization_barrier(values)


def order_blocks(place, plane, out, sems):
    xh, xl, z = place[0], place[1], place[2]
    half = plane.shape[2] // 2
    copies = []
    for r in range(8):
        at = lax.rem(z + 8 - r, 8)
        y, core = lax.div(at, 2), lax.rem(at, 2)
        for e in range(2):
            for b in range(2):
                device = (lax.rem(xh + e, 2) * 2 + lax.rem(xl + b, 2)) * 4 + y
                copy = pltpu.make_async_copy(
                    plane.at[device, :, pl.ds(pl.multiple_of(core * half, half), half)],
                    out.at[e, :, pl.ds((2 * r + b) * half, half)],
                    sems.at[len(copies)],
                )
                copy.start()
                copies.append(copy)
    for copy in copies:
        copy.wait()


def tokens_of_core(tokens):
    core = lax.axis_index("core")
    half = tokens.shape[1] // 2
    mine, other = swap_if(core == 1, tokens[:, :half], tokens[:, half:])
    received = exchange(other, "core", 1, 2)
    return jnp.concatenate(swap_if(core == 1, mine, received), axis=1)


def order_tokens(plane, rows):
    place = jnp.stack([lax.axis_index(name) for name in ("xh", "xl", "z")])
    features = plane.shape[2]
    ordered = pl.pallas_call(
        order_blocks,
        in_specs=[pl.BlockSpec(memory_space=pltpu.SMEM), pl.BlockSpec(memory_space=pl.ANY)],
        out_specs=pl.BlockSpec(memory_space=pl.ANY),
        out_shape=jax.ShapeDtypeStruct((2, rows, 8 * features), plane.dtype),
        scratch_shapes=[pltpu.SemaphoreType.DMA((32,))],
        cost_estimate=pl.CostEstimate(
            flops=0, transcendentals=0, bytes_accessed=4 * 16 * rows * features
        ),
    )(place, plane)
    return ordered.reshape(2 * rows, 8 * features)


def along_z(value, shift):
    return lax.ppermute(value, "z", [(i, (i + shift) % 8) for i in range(8)])


def step_along_z(step, up, down):
    if step == 4:
        half = up.shape[0] // 2
        up, down = up[:half], down[half:]
    return along_z(up, 1), along_z(down, -1)


def product(gathered, blocks, half):
    total = 0
    for block, piece in blocks:
        features = gathered[:, block * half : block * half + piece.shape[0]]
        total += jnp.dot(features, piece, preferred_element_type=jnp.float32)
    return total


def swapped(part):
    xh, xl, core = (lax.axis_index(name) for name in ("xh", "xl", "core"))
    half = part.shape[0] // 2
    first, second = swap_if(xh == 1, part[:half], part[half:])
    turned = lax.ppermute(first, ("xh", "core"), TURN)
    crossed = lax.ppermute(second, ("xh", "core"), CROSS)
    return jnp.concatenate(swap_if(xl != core, turned, crossed))


def activate(total):
    rows = total.shape[0] // 2
    core = lax.axis_index("core")
    kept, given = swap_if(core == 1, total[:rows], total[rows:])
    total = kept + exchange(given, "core", 1, 2)
    return jax.nn.silu(total).astype(jnp.bfloat16)


def home(out):
    return lax.ppermute(out, ("xh", "core"), HOME)


def on_device(tokens, weight):
    rows = tokens.shape[0]
    half = weight.shape[0] // 2
    w0, w1, w2, w3 = WIDTHS
    parts = [weight[:, :w0], weight[:, w0 : w0 + w1], weight[:, w0 + w1 :]]
    near = tokens_of_core(tokens)
    near, parts[0] = together(near, parts[0])
    plane = lax.all_gather(near[None], ("xh", "xl", "y"), axis=0, tiled=True)
    front = [None] * 4
    blocks = [None] * 4
    outs = [None] * 4

    def begin(chunk, value):
        front[chunk] = (value, value)
        blocks[chunk] = [(0, value)]

    def advance(chunk, step):
        up, down = together(*step_along_z(step, *front[chunk]))
        front[chunk] = (up, down)
        if step == 4:
            blocks[chunk] += [(8, up), (9, down)]
        else:
            blocks[chunk] += [(2 * step, up), (2 * (8 - step), down)]

    mine = swapped(parts[0])
    mine, parts[1] = together(mine, parts[1])
    begin(0, mine)
    mine = swapped(parts[1])
    mine, parts[2] = together(mine, parts[2])
    begin(1, mine)
    rest = swapped(parts[2])
    for step in range(1, 5):
        advance(0, step)
        advance(1, step)
    plane, *front[1] = together(plane, *front[1])
    gathered = order_tokens(plane, rows)
    for chunk, value in ((2, rest[:, :w2]), (3, rest[:, w2:])):
        up, down, value = together(*front[chunk - 2], value)
        blocks[chunk - 2][-2:] = [(8, up), (9, down)]
        begin(chunk, value)
    for step in range(1, 5):
        for chunk in (2, 3):
            early = chunk - 2
            if step == 2:
                outs[early] = product(gathered, blocks[early], half)
            if step == 3:
                outs[early] = activate(outs[early])
            if step == 4:
                outs[early] = home(outs[early])
            if step == 2 and chunk == 2:
                *front[2], outs[0], gathered = together(*front[2], outs[0], gathered)
            elif step > 1:
                *front[chunk], outs[early] = together(*front[chunk], outs[early])
            advance(chunk, step)
    for chunk in (2, 3):
        outs[chunk] = home(activate(product(gathered, blocks[chunk], half)))
    return jnp.concatenate(outs, axis=1)


def solution(mesh):
    fine = Mesh(mesh.devices.reshape(SIZES), AXES)
    placed = P(("xh", "z"), ("xl", "y", "core"))
    return jax.shard_map(
        on_device, mesh=fine, in_specs=(placed, placed), out_specs=placed, check_vma=False
    )
```

```python
import jax
import jax.numpy as jnp
from jax import lax
from jax.experimental import pallas as pl
from jax.experimental.pallas import tpu as pltpu
from jax.sharding import Mesh, PartitionSpec as P

AXES = ("xh", "z", "xl", "y", "core")
SIZES = (2, 8, 2, 4, 2)
WIDTHS = (768, 896)

TURN = [(h * 2 + c, c * 2 + h) for h in range(2) for c in range(2)]
CROSS = [(h * 2 + c, c * 2 + 1 - h) for h in range(2) for c in range(2)]
HOME = [(h * 2 + c, (h ^ c) * 2 + h) for h in range(2) for c in range(2)]


def exchange(value, axis, flip, size):
    return lax.ppermute(value, axis, [(i, i ^ flip) for i in range(size)])


def swap_if(flag, first, second):
    return jnp.where(flag, second, first), jnp.where(flag, first, second)


def together(*values):
    return lax.optimization_barrier(values)


def order_blocks(place, plane, out):
    half = plane.shape[2] // 2
    at = lax.rem(place[2] + 8 - pl.program_id(0), 8)
    y, core = lax.div(at, 2), lax.rem(at, 2)
    for e in range(2):
        for b in range(2):
            device = (lax.rem(place[0] + e, 2) * 2 + lax.rem(place[1] + b, 2)) * 4 + y
            columns = pl.ds(pl.multiple_of(core * half, half), half)
            out[e, :, b * half : (b + 1) * half] = plane[device, :, columns]


def tokens_of_core(tokens):
    core = lax.axis_index("core")
    half = tokens.shape[1] // 2
    mine, other = swap_if(core == 1, tokens[:, :half], tokens[:, half:])
    received = exchange(other, "core", 1, 2)
    return jnp.concatenate(swap_if(core == 1, mine, received), axis=1)


def order_tokens(plane, rows):
    place = jnp.stack([lax.axis_index(name) for name in ("xh", "xl", "z")])
    features = plane.shape[2]
    ordered = pl.pallas_call(
        order_blocks,
        grid=(8,),
        in_specs=[
            pl.BlockSpec(memory_space=pltpu.SMEM),
            pl.BlockSpec(plane.shape, lambda r: (0, 0, 0)),
        ],
        out_specs=pl.BlockSpec((2, rows, features), lambda r: (0, 0, r)),
        out_shape=jax.ShapeDtypeStruct((2, rows, 8 * features), plane.dtype),
        compiler_params=pltpu.CompilerParams(vmem_limit_bytes=32 * 2**20),
        cost_estimate=pl.CostEstimate(
            flops=0, transcendentals=0, bytes_accessed=4 * 16 * rows * features
        ),
    )(place, plane)
    return ordered.reshape(2 * rows, 8 * features)


def along_z(value, shift):
    return lax.ppermute(value, "z", [(i, (i + shift) % 8) for i in range(8)])


def step_along_z(step, up, down):
    if step == 4:
        half = up.shape[0] // 2
        up, down = up[:half], down[half:]
    return along_z(up, 1), along_z(down, -1)


def product(gathered, blocks, half):
    total = 0
    for block, piece in blocks:
        features = gathered[:, block * half : block * half + piece.shape[0]]
        total += jnp.dot(features, piece, preferred_element_type=jnp.float32)
    return total


def swapped(part):
    xh, xl, core = (lax.axis_index(name) for name in ("xh", "xl", "core"))
    half = part.shape[0] // 2
    first, second = swap_if(xh == 1, part[:half], part[half:])
    turned = lax.ppermute(first, ("xh", "core"), TURN)
    crossed = lax.ppermute(second, ("xh", "core"), CROSS)
    return jnp.concatenate(swap_if(xl != core, turned, crossed))


def activate(total):
    rows = total.shape[0] // 2
    core = lax.axis_index("core")
    kept, given = swap_if(core == 1, total[:rows], total[rows:])
    total = kept + exchange(given, "core", 1, 2)
    return jax.nn.silu(total).astype(jnp.bfloat16)


def home(out):
    return lax.ppermute(out, ("xh", "core"), HOME)


def on_device(tokens, weight):
    rows = tokens.shape[0]
    half = weight.shape[0] // 2
    parts = [weight[:, : WIDTHS[0]], weight[:, WIDTHS[0] :]]
    near = tokens_of_core(tokens)
    near, parts[0] = together(near, parts[0])
    plane = lax.all_gather(near[None], ("xh", "xl", "y"), axis=0, tiled=True)
    mine = swapped(parts[0])
    mine, parts[1] = together(mine, parts[1])
    mine = [mine, swapped(parts[1])]
    front = [(value, value) for value in mine]
    blocks = [[(0, value)] for value in mine]
    totals = [0, 0]
    gathered = None
    for step in range(1, 5):
        for chunk in range(2):
            if step == 2 and chunk:
                gathered, *front[1] = together(order_tokens(plane, rows), *front[1])
            if step > 2:
                totals[chunk] += product(gathered, blocks[chunk][:-2], half)
                blocks[chunk] = blocks[chunk][-2:]
                *front[chunk], totals[chunk] = together(*front[chunk], totals[chunk])
                blocks[chunk] = [(blocks[chunk][i][0], front[chunk][i]) for i in range(2)]
            up, down = together(*step_along_z(step, *front[chunk]))
            front[chunk] = (up, down)
            if step == 4:
                blocks[chunk] += [(8, up), (9, down)]
            else:
                blocks[chunk] += [(2 * step, up), (2 * (8 - step), down)]
    outs = [
        home(activate(totals[chunk] + product(gathered, blocks[chunk], half))) for chunk in range(2)
    ]
    return jnp.concatenate(outs, axis=1)


def solution(mesh):
    fine = Mesh(mesh.devices.reshape(SIZES), AXES)
    placed = P(("xh", "z"), ("xl", "y", "core"))
    return jax.shard_map(
        on_device, mesh=fine, in_specs=(placed, placed), out_specs=placed, check_vma=False
    )
```

```python
import jax
import jax.numpy as jnp
from jax import lax
from jax.experimental import pallas as pl
from jax.experimental.pallas import tpu as pltpu
from jax.sharding import Mesh, PartitionSpec as P

AXES = ("xh", "z", "xl", "y", "core")
SIZES = (2, 8, 2, 4, 2)
WIDTHS = (896, 768)

TURN = [(h * 2 + c, c * 2 + h) for h in range(2) for c in range(2)]
CROSS = [(h * 2 + c, c * 2 + 1 - h) for h in range(2) for c in range(2)]
HOME = [(h * 2 + c, (h ^ c) * 2 + h) for h in range(2) for c in range(2)]


def exchange(value, axis, flip, size):
    return lax.ppermute(value, axis, [(i, i ^ flip) for i in range(size)])


def swap_if(flag, first, second):
    return jnp.where(flag, second, first), jnp.where(flag, first, second)


def together(*values):
    return lax.optimization_barrier(values)


def order_blocks(place, plane, out):
    half = plane.shape[2] // 2
    at = lax.rem(place[2] + 8 - pl.program_id(0), 8)
    y, core = lax.div(at, 2), lax.rem(at, 2)
    for e in range(2):
        for b in range(2):
            device = (lax.rem(place[0] + e, 2) * 2 + lax.rem(place[1] + b, 2)) * 4 + y
            columns = pl.ds(pl.multiple_of(core * half, half), half)
            out[e, :, b * half : (b + 1) * half] = plane[device, :, columns]


def tokens_of_core(tokens):
    core = lax.axis_index("core")
    half = tokens.shape[1] // 2
    mine, other = swap_if(core == 1, tokens[:, :half], tokens[:, half:])
    received = exchange(other, "core", 1, 2)
    return jnp.concatenate(swap_if(core == 1, mine, received), axis=1)


def order_tokens(plane, rows):
    place = jnp.stack([lax.axis_index(name) for name in ("xh", "xl", "z")])
    features = plane.shape[2]
    ordered = pl.pallas_call(
        order_blocks,
        grid=(8,),
        in_specs=[
            pl.BlockSpec(memory_space=pltpu.SMEM),
            pl.BlockSpec(plane.shape, lambda r: (0, 0, 0)),
        ],
        out_specs=pl.BlockSpec((2, rows, features), lambda r: (0, 0, r)),
        out_shape=jax.ShapeDtypeStruct((2, rows, 8 * features), plane.dtype),
        compiler_params=pltpu.CompilerParams(vmem_limit_bytes=32 * 2**20),
        cost_estimate=pl.CostEstimate(
            flops=0, transcendentals=0, bytes_accessed=4 * 16 * rows * features
        ),
    )(place, plane)
    return ordered.reshape(2 * rows, 8 * features)


def along_z(value, shift):
    return lax.ppermute(value, "z", [(i, (i + shift) % 8) for i in range(8)])


def step_along_z(step, up, down):
    if step == 4:
        half = up.shape[0] // 2
        up, down = up[:half], down[half:]
    return along_z(up, 1), along_z(down, -1)


def product(gathered, blocks, half):
    total = 0
    for block, piece in blocks:
        features = gathered[:, block * half : block * half + piece.shape[0]]
        total += jnp.dot(features, piece, preferred_element_type=jnp.float32)
    return total


def swapped(part):
    xh, xl, core = (lax.axis_index(name) for name in ("xh", "xl", "core"))
    half = part.shape[0] // 2
    first, second = swap_if(xh == 1, part[:half], part[half:])
    turned = lax.ppermute(first, ("xh", "core"), TURN)
    crossed = lax.ppermute(second, ("xh", "core"), CROSS)
    return jnp.concatenate(swap_if(xl != core, turned, crossed))


def activate(total):
    rows = total.shape[0] // 2
    core = lax.axis_index("core")
    kept, given = swap_if(core == 1, total[:rows], total[rows:])
    total = kept + exchange(given, "core", 1, 2)
    return jax.nn.silu(total).astype(jnp.bfloat16)


def home(out):
    return lax.ppermute(out, ("xh", "core"), HOME)


def on_device(tokens, weight):
    rows = tokens.shape[0]
    half = weight.shape[0] // 2
    parts = [weight[:, : WIDTHS[0]], weight[:, WIDTHS[0] :]]
    near = tokens_of_core(tokens)
    plane = lax.all_to_all(
        jnp.broadcast_to(near, (16, *near.shape)), ("xh", "xl", "y"), 0, 0, tiled=True
    )
    mine = swapped(parts[0])
    mine, parts[1] = together(mine, parts[1])
    mine = [mine, swapped(parts[1])]
    front = [(value, value) for value in mine]
    blocks = [[(0, value)] for value in mine]
    totals = [0, 0]
    outs = [None, None]

    def fold(chunk, count):
        totals[chunk] += product(gathered, blocks[chunk][:count], half)
        del blocks[chunk][:count]

    for step in range(1, 5):
        for chunk in range(2):
            if step == 3 and not chunk:
                gathered, *front[0] = together(order_tokens(plane, rows), *front[0])
            if step == 4 and chunk:
                fold(0, 9)
                outs[0] = home(activate(totals[0]))
            up, down = step_along_z(step, *front[chunk])
            if step == 4 and chunk:
                up, down, outs[0] = together(up, down, outs[0])
            else:
                up, down = together(up, down)
            front[chunk] = (up, down)
            if step == 4:
                blocks[chunk] += [(8, up), (9, down)]
            else:
                blocks[chunk] += [(2 * step, up), (2 * (8 - step), down)]
    fold(1, 9)
    outs[1] = home(activate(totals[1]))
    return jnp.concatenate(outs, axis=1)


def solution(mesh):
    fine = Mesh(mesh.devices.reshape(SIZES), AXES)
    placed = P(("xh", "z"), ("xl", "y", "core"))
    return jax.shard_map(
        on_device, mesh=fine, in_specs=(placed, placed), out_specs=placed, check_vma=False
    )
```

```python
import jax
import jax.numpy as jnp
from jax import lax
from jax.experimental import pallas as pl
from jax.experimental.pallas import tpu as pltpu
from jax.sharding import Mesh, PartitionSpec as P

AXES = ("xh", "z", "xl", "y", "core")
SIZES = (2, 8, 2, 4, 2)
WIDTHS = (896, 768)

TURN = [(h * 2 + c, c * 2 + h) for h in range(2) for c in range(2)]
CROSS = [(h * 2 + c, c * 2 + 1 - h) for h in range(2) for c in range(2)]
HOME = [(h * 2 + c, (h ^ c) * 2 + h) for h in range(2) for c in range(2)]


def exchange(value, axis, flip, size):
    return lax.ppermute(value, axis, [(i, i ^ flip) for i in range(size)])


def swap_if(flag, first, second):
    return jnp.where(flag, second, first), jnp.where(flag, first, second)


def together(*values):
    return lax.optimization_barrier(values)


def tokens_of_core(tokens):
    core = lax.axis_index("core")
    half = tokens.shape[1] // 2
    mine, other = swap_if(core == 1, tokens[:, :half], tokens[:, half:])
    received = exchange(other, "core", 1, 2)
    near = swap_if(core == 1, mine, received)
    far = exchange(jnp.concatenate(near, axis=1), "xl", 1, 2)
    return jnp.concatenate([near[0], far[:, :half], near[1], far[:, half:]], axis=1)


def along_y(value, shift):
    return lax.ppermute(value, "y", [(i, (i + shift) % 4) for i in range(4)])


def gather_along_y(both):
    up, down = along_y(both, 1), along_y(both, -1)
    return [both, up, down, along_y(up[0], 1), along_y(down[1], -1)]


def order_blocks(place, here, up, down, far_up, far_down, out):
    width = out.shape[2]
    at = lax.rem(place[0] + 8 - pl.program_id(0), 8)
    columns = pl.ds(pl.multiple_of(lax.rem(at, 2) * width, width), width)
    shift = lax.rem(lax.div(at, 2) + 4 - place[1], 4)
    for s, piece in ((0, here), (3, up), (1, down)):

        @pl.when(shift == s)
        def copy():
            for e in range(2):
                out[e] = piece[e, :, columns]

    @pl.when(shift == 2)
    def copy_far():
        out[0] = far_up[:, columns]
        out[1] = far_down[:, columns]


def order_tokens(pieces):
    two, rows, columns = pieces[0].shape
    place = jnp.stack([lax.axis_index("z"), lax.axis_index("y")])
    ordered = pl.pallas_call(
        order_blocks,
        grid=(8,),
        in_specs=[pl.BlockSpec(memory_space=pltpu.SMEM)]
        + [pl.BlockSpec(piece.shape, lambda r, n=piece.ndim: (0,) * n) for piece in pieces],
        out_specs=pl.BlockSpec((two, rows, columns // 2), lambda r: (0, 0, r)),
        out_shape=jax.ShapeDtypeStruct((two, rows, 4 * columns), pieces[0].dtype),
        compiler_params=pltpu.CompilerParams(vmem_limit_bytes=40 * 2**20),
        cost_estimate=pl.CostEstimate(
            flops=0, transcendentals=0, bytes_accessed=16 * two * rows * columns
        ),
    )(place, *pieces)
    return ordered.reshape(two * rows, 4 * columns)


def along_z(value, shift):
    return lax.ppermute(value, "z", [(i, (i + shift) % 8) for i in range(8)])


def step_along_z(step, up, down):
    if step == 4:
        half = up.shape[0] // 2
        up, down = up[:half], down[half:]
    return along_z(up, 1), along_z(down, -1)


def product(gathered, blocks, half):
    total = 0
    for block, piece in blocks:
        features = gathered[:, block * half : block * half + piece.shape[0]]
        total += jnp.dot(features, piece, preferred_element_type=jnp.float32)
    return total


def swapped(weight, also):
    xh, xl, core = (lax.axis_index(name) for name in ("xh", "xl", "core"))
    half = weight.shape[0] // 2
    first, second = swap_if(xh == 1, weight[:half], weight[half:])
    turned = lax.ppermute(first, ("xh", "core"), TURN)
    crossed = lax.ppermute(second, ("xh", "core"), CROSS)
    also, turned, crossed = together(also, turned, crossed)
    return jnp.concatenate(swap_if(xl != core, turned, crossed)), also


def activate(total):
    rows = total.shape[0] // 2
    core = lax.axis_index("core")
    kept, given = swap_if(core == 1, total[:rows], total[rows:])
    total = kept + exchange(given, "core", 1, 2)
    return jax.nn.silu(total).astype(jnp.bfloat16)


def home(out):
    return lax.ppermute(out, ("xh", "core"), HOME)


def on_device(tokens, weight):
    half = weight.shape[0] // 2
    piece = tokens_of_core(tokens)
    beside = exchange(piece, "xh", 1, 2)
    mine, piece = swapped(weight, piece)
    both = jnp.stack([piece, beside])
    pieces = gather_along_y(both)
    up = down = mine
    blocks = [(0, mine)]
    for step in range(1, 4):
        up, down = together(*step_along_z(step, up, down))
        blocks += [(2 * step, up), (2 * (8 - step), down)]
    gathered = order_tokens(pieces)
    early = product(gathered, blocks[:5], half)
    early, up, down = together(early, up, down)
    early += product(gathered, [(6, up), (10, down)], half)
    up, down, early = together(*step_along_z(4, up, down), early)
    cut = WIDTHS[0]
    outs = []
    for columns in (slice(0, cut), slice(cut, None)):
        last = product(gathered, ((8, up[:, columns]), (9, down[:, columns])), half)
        outs.append(home(activate(early[:, columns] + last)))
    return jnp.concatenate(outs, axis=1)


def solution(mesh):
    fine = Mesh(mesh.devices.reshape(SIZES), AXES)
    placed = P(("xh", "z"), ("xl", "y", "core"))
    return jax.shard_map(
        on_device, mesh=fine, in_specs=(placed, placed), out_specs=placed, check_vma=False
    )
```

```python
import jax
import jax.numpy as jnp
from jax import lax
from jax.experimental import pallas as pl
from jax.experimental.pallas import tpu as pltpu
from jax.sharding import Mesh, PartitionSpec as P

AXES = ("xh", "z", "xl", "y", "core")
SIZES = (2, 8, 2, 4, 2)
WIDTHS = (896, 768)

TURN = [(h * 2 + c, c * 2 + h) for h in range(2) for c in range(2)]
CROSS = [(h * 2 + c, c * 2 + 1 - h) for h in range(2) for c in range(2)]
HOME = [(h * 2 + c, (h ^ c) * 2 + h) for h in range(2) for c in range(2)]


def exchange(value, axis, flip, size):
    return lax.ppermute(value, axis, [(i, i ^ flip) for i in range(size)])


def swap_if(flag, first, second):
    return jnp.where(flag, second, first), jnp.where(flag, first, second)


def together(*values):
    return lax.optimization_barrier(values)


def tokens_of_core(tokens):
    core = lax.axis_index("core")
    half = tokens.shape[1] // 2
    mine, other = swap_if(core == 1, tokens[:, :half], tokens[:, half:])
    received = exchange(other, "core", 1, 2)
    near = swap_if(core == 1, mine, received)
    far = exchange(jnp.concatenate(near, axis=1), "xl", 1, 2)
    return jnp.concatenate([near[0], far[:, :half], near[1], far[:, half:]], axis=1)


def along_y(value, shift):
    return lax.ppermute(value, "y", [(i, (i + shift) % 4) for i in range(4)])


def gather_along_y(both):
    up, down = along_y(both, 1), along_y(both, -1)
    return [both, up, down, along_y(up[0], 1), along_y(down[1], -1)]


def order_blocks(place, here, up, down, far_up, far_down, out):
    width = out.shape[2]
    at = lax.rem(place[0] + 8 - pl.program_id(0), 8)
    columns = pl.ds(pl.multiple_of(lax.rem(at, 2) * width, width), width)
    shift = lax.rem(lax.div(at, 2) + 4 - place[1], 4)
    for s, piece in ((0, here), (3, up), (1, down)):

        @pl.when(shift == s)
        def copy():
            for e in range(2):
                out[e] = piece[e, :, columns]

    @pl.when(shift == 2)
    def copy_far():
        out[0] = far_up[:, columns]
        out[1] = far_down[:, columns]


def order_tokens(pieces):
    two, rows, columns = pieces[0].shape
    place = jnp.stack([lax.axis_index("z"), lax.axis_index("y")])
    ordered = pl.pallas_call(
        order_blocks,
        grid=(8,),
        in_specs=[pl.BlockSpec(memory_space=pltpu.SMEM)]
        + [pl.BlockSpec(piece.shape, lambda r, n=piece.ndim: (0,) * n) for piece in pieces],
        out_specs=pl.BlockSpec((two, rows, columns // 2), lambda r: (0, 0, r)),
        out_shape=jax.ShapeDtypeStruct((two, rows, 4 * columns), pieces[0].dtype),
        compiler_params=pltpu.CompilerParams(vmem_limit_bytes=40 * 2**20),
        cost_estimate=pl.CostEstimate(
            flops=0, transcendentals=0, bytes_accessed=16 * two * rows * columns
        ),
    )(place, *pieces)
    return ordered.reshape(two * rows, 4 * columns)


def along_z(value, shift):
    return lax.ppermute(value, "z", [(i, (i + shift) % 8) for i in range(8)])


def step_along_z(step, up, down):
    if step == 4:
        half = up.shape[0] // 2
        up, down = up[:half], down[half:]
    return along_z(up, 1), along_z(down, -1)


def product(gathered, blocks, half):
    total = 0
    for block, piece in blocks:
        features = gathered[:, block * half : block * half + piece.shape[0]]
        total += jnp.dot(features, piece, preferred_element_type=jnp.float32)
    return total


def swapped(weight, *also):
    xh, xl, core = (lax.axis_index(name) for name in ("xh", "xl", "core"))
    half = weight.shape[0] // 2
    first, second = swap_if(xh == 1, weight[:half], weight[half:])
    turned = lax.ppermute(first, ("xh", "core"), TURN)
    crossed = lax.ppermute(second, ("xh", "core"), CROSS)
    *also, turned, crossed = together(*also, turned, crossed)
    return jnp.concatenate(swap_if(xl != core, turned, crossed)), *also


def activate(total):
    rows = total.shape[0] // 2
    core = lax.axis_index("core")
    kept, given = swap_if(core == 1, total[:rows], total[rows:])
    total = kept + exchange(given, "core", 1, 2)
    return jax.nn.silu(total).astype(jnp.bfloat16)


def home(out):
    return lax.ppermute(out, ("xh", "core"), HOME)


def on_device(tokens, weight):
    half = weight.shape[0] // 2
    cut = WIDTHS[0]
    piece = tokens_of_core(tokens)
    beside = exchange(piece, "xh", 1, 2)
    mine, piece = swapped(weight[:, :cut], piece)
    rest, mine = together(weight[:, cut:], mine)
    up, down = together(*step_along_z(1, mine, mine))
    (rest,) = swapped(rest)
    rest_up, rest_down = together(*step_along_z(1, rest, rest))
    both = jnp.stack([piece, beside])
    pieces = gather_along_y(both)
    mine = jnp.concatenate([mine, rest], axis=1)
    up = jnp.concatenate([up, rest_up], axis=1)
    down = jnp.concatenate([down, rest_down], axis=1)
    blocks = [(0, mine), (2, up), (14, down)]
    for step in range(2, 4):
        up, down = together(*step_along_z(step, up, down))
        if step == 2:
            tied_up, tied_down, *pieces = together(up, down, *pieces)
            blocks += [(2 * step, tied_up), (2 * (8 - step), tied_down)]
    gathered = order_tokens(pieces)
    early = product(gathered, blocks[:5], half)
    early, up, down = together(early, up, down)
    early += product(gathered, [(6, up), (10, down)], half)
    up, down, early = together(*step_along_z(4, up, down), early)
    outs = []
    for columns in (slice(0, cut), slice(cut, None)):
        last = product(gathered, ((8, up[:, columns]), (9, down[:, columns])), half)
        outs.append(home(activate(early[:, columns] + last)))
    return jnp.concatenate(outs, axis=1)


def solution(mesh):
    fine = Mesh(mesh.devices.reshape(SIZES), AXES)
    placed = P(("xh", "z"), ("xl", "y", "core"))
    return jax.shard_map(
        on_device, mesh=fine, in_specs=(placed, placed), out_specs=placed, check_vma=False
    )
```

```python
import jax
import jax.numpy as jnp
from jax import lax
from jax.experimental import pallas as pl
from jax.experimental.pallas import tpu as pltpu
from jax.sharding import Mesh, PartitionSpec as P

AXES = ("xh", "z", "xl", "y", "core")
SIZES = (2, 8, 2, 4, 2)
FIRST = 768
LAST = 1024

TURN = [(h * 2 + c, c * 2 + h) for h in range(2) for c in range(2)]
CROSS = [(h * 2 + c, c * 2 + 1 - h) for h in range(2) for c in range(2)]
HOME = [(h * 2 + c, (h ^ c) * 2 + h) for h in range(2) for c in range(2)]


def exchange(value, axis, flip, size):
    return lax.ppermute(value, axis, [(i, i ^ flip) for i in range(size)])


def swap_if(flag, first, second):
    return jnp.where(flag, second, first), jnp.where(flag, first, second)


def together(*values):
    return lax.optimization_barrier(values)


def tokens_of_core(tokens):
    core = lax.axis_index("core")
    half = tokens.shape[1] // 2
    mine, other = swap_if(core == 1, tokens[:, :half], tokens[:, half:])
    return jnp.concatenate(swap_if(core == 1, mine, exchange(other, "core", 1, 2)), axis=1)


def tokens_of_pair(near):
    half = near.shape[1] // 2
    far = exchange(near, "xl", 1, 2)
    return jnp.concatenate([near[:, :half], far[:, :half], near[:, half:], far[:, half:]], axis=1)


def along_y(value, shift):
    return lax.ppermute(value, "y", [(i, (i + shift) % 4) for i in range(4)])


def gather_along_y(both):
    up, down = along_y(both, 1), along_y(both, -1)
    return [both, up, down, along_y(up[0], 1), along_y(down[1], -1)]


def order_blocks(place, here, up, down, far_up, far_down, out):
    width = out.shape[2]
    at = lax.rem(place[0] + 8 - pl.program_id(0), 8)
    columns = pl.ds(pl.multiple_of(lax.rem(at, 2) * width, width), width)
    shift = lax.rem(lax.div(at, 2) + 4 - place[1], 4)
    for s, piece in ((0, here), (3, up), (1, down)):

        @pl.when(shift == s)
        def copy():
            for e in range(2):
                out[e] = piece[e, :, columns]

    @pl.when(shift == 2)
    def copy_far():
        out[0] = far_up[:, columns]
        out[1] = far_down[:, columns]


def order_tokens(pieces):
    two, rows, columns = pieces[0].shape
    place = jnp.stack([lax.axis_index("z"), lax.axis_index("y")])
    ordered = pl.pallas_call(
        order_blocks,
        grid=(8,),
        in_specs=[pl.BlockSpec(memory_space=pltpu.SMEM)]
        + [pl.BlockSpec(piece.shape, lambda r, n=piece.ndim: (0,) * n) for piece in pieces],
        out_specs=pl.BlockSpec((two, rows, columns // 2), lambda r: (0, 0, r)),
        out_shape=jax.ShapeDtypeStruct((two, rows, 4 * columns), pieces[0].dtype),
        compiler_params=pltpu.CompilerParams(vmem_limit_bytes=40 * 2**20),
        cost_estimate=pl.CostEstimate(
            flops=0, transcendentals=0, bytes_accessed=16 * two * rows * columns
        ),
    )(place, *pieces)
    return ordered.reshape(two * rows, 4 * columns)


def along_z(value, shift):
    return lax.ppermute(value, "z", [(i, (i + shift) % 8) for i in range(8)])


def step_along_z(step, up, down):
    if step == 4:
        half = up.shape[0] // 2
        up, down = up[:half], down[half:]
    return along_z(up, 1), along_z(down, -1)


def product(gathered, blocks, half):
    total = 0
    for block, piece in blocks:
        features = gathered[:, block * half : block * half + piece.shape[0]]
        total += jnp.dot(features, piece, preferred_element_type=jnp.float32)
    return total


def swapped(weight):
    xh, xl, core = (lax.axis_index(name) for name in ("xh", "xl", "core"))
    half = weight.shape[0] // 2
    first, second = swap_if(xh == 1, weight[:half], weight[half:])
    turned = lax.ppermute(first, ("xh", "core"), TURN)
    crossed = lax.ppermute(second, ("xh", "core"), CROSS)
    return jnp.concatenate(swap_if(xl != core, turned, crossed))


def activate(total):
    rows = total.shape[0] // 2
    core = lax.axis_index("core")
    kept, given = swap_if(core == 1, total[:rows], total[rows:])
    total = kept + exchange(given, "core", 1, 2)
    return jax.nn.silu(total).astype(jnp.bfloat16)


def home(out):
    return lax.ppermute(out, ("xh", "core"), HOME)


def on_device(tokens, weight):
    half = weight.shape[0] // 2
    mine, tokens = together(swapped(weight[:, :FIRST]), tokens)
    up, down = together(*step_along_z(1, mine, mine))
    near, rest = together(tokens_of_core(tokens), weight[:, FIRST:])
    rest = swapped(rest)
    rest_up, rest_down = together(*step_along_z(1, rest, rest))
    piece, up, down = together(tokens_of_pair(near), up, down)
    beside = exchange(piece, "xh", 1, 2)
    both = jnp.stack([piece, beside])
    pieces = gather_along_y(both)
    mine = jnp.concatenate([mine, rest], axis=1)
    up = jnp.concatenate([up, rest_up], axis=1)
    down = jnp.concatenate([down, rest_down], axis=1)
    blocks = [(0, mine), (2, up), (14, down)]
    for step in range(2, 4):
        up, down = together(*step_along_z(step, up, down))
        if step == 2:
            tied_up, tied_down, *pieces = together(up, down, *pieces)
            blocks += [(2 * step, tied_up), (2 * (8 - step), tied_down)]
    gathered = order_tokens(pieces)
    early = product(gathered, blocks[:5], half)
    early, up, down = together(early, up, down)
    early += product(gathered, [(6, up), (10, down)], half)
    ends = [
        step_along_z(4, up[:, columns], down[:, columns])
        for columns in (slice(0, LAST), slice(LAST, None))
    ]
    up, down, early = together(*ends[0], early)
    first = activate(early[:, :LAST] + product(gathered, ((8, up), (9, down)), half))
    up, down, first = together(*ends[1], first)
    second = activate(early[:, LAST:] + product(gathered, ((8, up), (9, down)), half))
    return jnp.concatenate([home(first), home(second)], axis=1)


def solution(mesh):
    fine = Mesh(mesh.devices.reshape(SIZES), AXES)
    placed = P(("xh", "z"), ("xl", "y", "core"))
    return jax.shard_map(
        on_device, mesh=fine, in_specs=(placed, placed), out_specs=placed, check_vma=False
    )
```

```python
import jax
import jax.numpy as jnp
from jax import lax
from jax.experimental import pallas as pl
from jax.experimental.pallas import tpu as pltpu
from jax.sharding import Mesh, PartitionSpec as P

AXES = ("xh", "z", "xl", "y", "core")
SIZES = (2, 8, 2, 4, 2)
FIRST = 768
LAST = 1024

TURN = [(h * 2 + c, c * 2 + h) for h in range(2) for c in range(2)]
CROSS = [(h * 2 + c, c * 2 + 1 - h) for h in range(2) for c in range(2)]
HOME = [(h * 2 + c, (h ^ c) * 2 + h) for h in range(2) for c in range(2)]


def exchange(value, axis, flip, size):
    return lax.ppermute(value, axis, [(i, i ^ flip) for i in range(size)])


def swap_if(flag, first, second):
    return jnp.where(flag, second, first), jnp.where(flag, first, second)


def together(*values):
    return lax.optimization_barrier(values)


def tokens_of_core(tokens):
    core = lax.axis_index("core")
    half = tokens.shape[1] // 2
    mine, other = swap_if(core == 1, tokens[:, :half], tokens[:, half:])
    return jnp.concatenate(swap_if(core == 1, mine, exchange(other, "core", 1, 2)), axis=1)


def tokens_of_pair(near):
    half = near.shape[1] // 2
    far = exchange(near, "xl", 1, 2)
    return jnp.concatenate([near[:, :half], far[:, :half], near[:, half:], far[:, half:]], axis=1)


def along_y(value, shift):
    return lax.ppermute(value, "y", [(i, (i + shift) % 4) for i in range(4)])


def gather_along_y(both):
    up, down = along_y(both, 1), along_y(both, -1)
    return [both, up, down, along_y(up[0], 1), along_y(down[1], -1)]


def order_blocks(place, here, up, down, far_up, far_down, out):
    width = out.shape[2]
    at = lax.rem(place[0] + 8 - pl.program_id(0), 8)
    columns = pl.ds(pl.multiple_of(lax.rem(at, 2) * width, width), width)
    shift = lax.rem(lax.div(at, 2) + 4 - place[1], 4)
    for s, piece in ((0, here), (3, up), (1, down)):

        @pl.when(shift == s)
        def copy():
            for e in range(2):
                out[e] = piece[e, :, columns]

    @pl.when(shift == 2)
    def copy_far():
        out[0] = far_up[:, columns]
        out[1] = far_down[:, columns]


def order_tokens(pieces):
    two, rows, columns = pieces[0].shape
    place = jnp.stack([lax.axis_index("z"), lax.axis_index("y")])
    ordered = pl.pallas_call(
        order_blocks,
        grid=(8,),
        in_specs=[pl.BlockSpec(memory_space=pltpu.SMEM)]
        + [pl.BlockSpec(piece.shape, lambda r, n=piece.ndim: (0,) * n) for piece in pieces],
        out_specs=pl.BlockSpec((two, rows, columns // 2), lambda r: (0, 0, r)),
        out_shape=jax.ShapeDtypeStruct((two, rows, 4 * columns), pieces[0].dtype),
        compiler_params=pltpu.CompilerParams(vmem_limit_bytes=40 * 2**20),
        cost_estimate=pl.CostEstimate(
            flops=0, transcendentals=0, bytes_accessed=16 * two * rows * columns
        ),
    )(place, *pieces)
    return ordered.reshape(two * rows, 4 * columns)


def along_z(value, shift):
    return lax.ppermute(value, "z", [(i, (i + shift) % 8) for i in range(8)])


def step_along_z(up, down):
    return along_z(up, 1), along_z(down, -1)


def product(gathered, blocks, half):
    total = 0
    for block, piece in blocks:
        features = gathered[:, block * half : block * half + piece.shape[0]]
        total += jnp.dot(features, piece, preferred_element_type=jnp.float32)
    return total


def swapped(weight):
    xh, xl, core = (lax.axis_index(name) for name in ("xh", "xl", "core"))
    half = weight.shape[0] // 2
    first, second = swap_if(xh == 1, weight[:half], weight[half:])
    turned = lax.ppermute(first, ("xh", "core"), TURN)
    crossed = lax.ppermute(second, ("xh", "core"), CROSS)
    return jnp.concatenate(swap_if(xl != core, turned, crossed))


def activate(total):
    rows = total.shape[0] // 2
    core = lax.axis_index("core")
    kept, given = swap_if(core == 1, total[:rows], total[rows:])
    total = kept + exchange(given, "core", 1, 2)
    return jax.nn.silu(total).astype(jnp.bfloat16)


def home(out):
    return lax.ppermute(out, ("xh", "core"), HOME)


def on_device(tokens, weight):
    half = weight.shape[0] // 2
    mine, tokens = together(swapped(weight[:, :FIRST]), tokens)
    up, down = together(*step_along_z(mine, mine))
    near, rest = together(tokens_of_core(tokens), weight[:, FIRST:])
    rest = swapped(rest)
    rest_up, rest_down = together(*step_along_z(rest, rest))
    piece, up, down = together(tokens_of_pair(near), up, down)
    beside = exchange(piece, "xh", 1, 2)
    both = jnp.stack([piece, beside])
    pieces = gather_along_y(both)
    mine = jnp.concatenate([mine, rest], axis=1)
    up = jnp.concatenate([up, rest_up], axis=1)
    down = jnp.concatenate([down, rest_down], axis=1)
    blocks = [(0, mine), (2, up), (14, down)]
    for step in range(2, 4):
        up, down = together(*step_along_z(up, down))
        if step == 2:
            tied_up, tied_down, *pieces = together(up, down, *pieces)
            blocks += [(2 * step, tied_up), (2 * (8 - step), tied_down)]
    gathered = order_tokens(pieces)
    early = product(gathered, blocks[:5], half)
    early, up, down = together(early, up, down)
    quarter = slice(0, half), slice(half, None)
    sent = [
        (up[quarter[0], columns], down[quarter[1], columns])
        for columns in (slice(0, LAST), slice(LAST, None))
    ]
    (*sent[0], up, down) = together(*sent[0], up, down)
    early += product(gathered, [(6, up), (10, down)], half)
    ends = [step_along_z(*pair) for pair in sent]
    up, down, early = together(*ends[0], early)
    total = early[:, :LAST] + product(gathered, ((8, up), (9, down)), half)
    total, up, down = together(total, *ends[1])
    first = home(activate(total))
    second = activate(early[:, LAST:] + product(gathered, ((8, up), (9, down)), half))
    return jnp.concatenate([first, home(second)], axis=1)


def solution(mesh):
    fine = Mesh(mesh.devices.reshape(SIZES), AXES)
    placed = P(("xh", "z"), ("xl", "y", "core"))
    return jax.shard_map(
        on_device, mesh=fine, in_specs=(placed, placed), out_specs=placed, check_vma=False
    )
```

```python
import jax
import jax.numpy as jnp
from jax import lax
from jax.experimental import pallas as pl
from jax.experimental.pallas import tpu as pltpu
from jax.sharding import Mesh, PartitionSpec as P

AXES = ("xh", "z", "xl", "y", "core")
SIZES = (2, 8, 2, 4, 2)
FIRST = 768
LAST = 1024

TURN = [(h * 2 + c, c * 2 + h) for h in range(2) for c in range(2)]
CROSS = [(h * 2 + c, c * 2 + 1 - h) for h in range(2) for c in range(2)]
HOME = [(h * 2 + c, (h ^ c) * 2 + h) for h in range(2) for c in range(2)]


def exchange(value, axis, flip, size):
    return lax.ppermute(value, axis, [(i, i ^ flip) for i in range(size)])


def swap_if(flag, first, second):
    return jnp.where(flag, second, first), jnp.where(flag, first, second)


def together(*values):
    return lax.optimization_barrier(values)


def tokens_of_core(tokens):
    core = lax.axis_index("core")
    half = tokens.shape[1] // 2
    mine, other = swap_if(core == 1, tokens[:, :half], tokens[:, half:])
    return jnp.concatenate(swap_if(core == 1, mine, exchange(other, "core", 1, 2)), axis=1)


def tokens_of_pair(near):
    half = near.shape[1] // 2
    far = exchange(near, "xl", 1, 2)
    return jnp.concatenate([near[:, :half], far[:, :half], near[:, half:], far[:, half:]], axis=1)


def along_y(value, shift):
    return lax.ppermute(value, "y", [(i, (i + shift) % 4) for i in range(4)])


def gather_along_y(both):
    up, down = along_y(both, 1), along_y(both, -1)
    return [both, up, down, along_y(up[0], 1), along_y(down[1], -1)]


def order_blocks(place, here, up, down, far_up, far_down, out):
    width = out.shape[2]
    at = lax.rem(place[0] + 8 - pl.program_id(0), 8)
    columns = pl.ds(pl.multiple_of(lax.rem(at, 2) * width, width), width)
    shift = lax.rem(lax.div(at, 2) + 4 - place[1], 4)
    for s, piece in ((0, here), (3, up), (1, down)):

        @pl.when(shift == s)
        def copy():
            for e in range(2):
                out[e] = piece[e, :, columns]

    @pl.when(shift == 2)
    def copy_far():
        out[0] = far_up[:, columns]
        out[1] = far_down[:, columns]


def order_tokens(pieces):
    two, rows, columns = pieces[0].shape
    place = jnp.stack([lax.axis_index("z"), lax.axis_index("y")])
    ordered = pl.pallas_call(
        order_blocks,
        grid=(8,),
        in_specs=[pl.BlockSpec(memory_space=pltpu.SMEM)]
        + [pl.BlockSpec(piece.shape, lambda r, n=piece.ndim: (0,) * n) for piece in pieces],
        out_specs=pl.BlockSpec((two, rows, columns // 2), lambda r: (0, 0, r)),
        out_shape=jax.ShapeDtypeStruct((two, rows, 4 * columns), pieces[0].dtype),
        compiler_params=pltpu.CompilerParams(vmem_limit_bytes=40 * 2**20),
        cost_estimate=pl.CostEstimate(
            flops=0, transcendentals=0, bytes_accessed=16 * two * rows * columns
        ),
    )(place, *pieces)
    return ordered.reshape(two * rows, 4 * columns)


def along_z(value, shift):
    return lax.ppermute(value, "z", [(i, (i + shift) % 8) for i in range(8)])


def step_along_z(up, down):
    return along_z(up, 1), along_z(down, -1)


def product(gathered, blocks, half):
    total = 0
    for block, piece in blocks:
        features = gathered[:, block * half : block * half + piece.shape[0]]
        total += jnp.dot(features, piece, preferred_element_type=jnp.float32)
    return total


def swapped(weight):
    xh, xl, core = (lax.axis_index(name) for name in ("xh", "xl", "core"))
    half = weight.shape[0] // 2
    first, second = swap_if(xh == 1, weight[:half], weight[half:])
    turned = lax.ppermute(first, ("xh", "core"), TURN)
    crossed = lax.ppermute(second, ("xh", "core"), CROSS)
    return jnp.concatenate(swap_if(xl != core, turned, crossed))


def activate(total):
    rows = total.shape[0] // 2
    core = lax.axis_index("core")
    kept, given = swap_if(core == 1, total[:rows], total[rows:])
    total = kept + exchange(given, "core", 1, 2)
    return jax.nn.silu(total).astype(jnp.bfloat16)


def home(out):
    return lax.ppermute(out, ("xh", "core"), HOME)


def on_device(tokens, weight):
    half = weight.shape[0] // 2
    mine, tokens = together(swapped(weight[:, :FIRST]), tokens)
    up, down = together(*step_along_z(mine, mine))
    near, rest = together(tokens_of_core(tokens), weight[:, FIRST:])
    rest = swapped(rest)
    rest_up, rest_down = together(*step_along_z(rest, rest))
    piece, up, down = together(tokens_of_pair(near), up, down)
    beside = exchange(piece, "xh", 1, 2)
    both = jnp.stack([piece, beside])
    pieces = gather_along_y(both)
    mine = jnp.concatenate([mine, rest], axis=1)
    up = jnp.concatenate([up, rest_up], axis=1)
    down = jnp.concatenate([down, rest_down], axis=1)
    blocks = [(0, mine), (2, up), (14, down)]
    for step in range(2, 4):
        up, down = together(*step_along_z(up, down))
        if step == 2:
            tied_up, tied_down, *pieces = together(up, down, *pieces)
            blocks += [(2 * step, tied_up), (2 * (8 - step), tied_down)]
    gathered = order_tokens(pieces)
    early = product(gathered, blocks[:5], half)
    early, up, down = together(early, up, down)
    quarter = slice(0, half), slice(half, None)
    sent = [
        (up[quarter[0], columns], down[quarter[1], columns])
        for columns in (slice(0, LAST), slice(LAST, None))
    ]
    ends = [step_along_z(*pair) for pair in sent]
    late_up, late_down, up, down = together(up, down, *ends[0])
    early += product(gathered, [(6, late_up), (10, late_down)], half)
    total = early[:, :LAST] + product(gathered, ((8, up), (9, down)), half)
    total, up, down = together(total, *ends[1])
    first = home(activate(total))
    second = activate(early[:, LAST:] + product(gathered, ((8, up), (9, down)), half))
    return jnp.concatenate([first, home(second)], axis=1)


def solution(mesh):
    fine = Mesh(mesh.devices.reshape(SIZES), AXES)
    placed = P(("xh", "z"), ("xl", "y", "core"))
    return jax.shard_map(
        on_device, mesh=fine, in_specs=(placed, placed), out_specs=placed, check_vma=False
    )
```

```python
import jax
import jax.numpy as jnp
from jax import lax
from jax.experimental import pallas as pl
from jax.experimental.pallas import tpu as pltpu
from jax.sharding import Mesh, PartitionSpec as P

AXES = ("xh", "z", "xl", "y", "core")
SIZES = (2, 8, 2, 4, 2)
FIRST = 768
LAST = 1024

TURN = [(h * 2 + c, c * 2 + h) for h in range(2) for c in range(2)]
CROSS = [(h * 2 + c, c * 2 + 1 - h) for h in range(2) for c in range(2)]
HOME = [(h * 2 + c, (h ^ c) * 2 + h) for h in range(2) for c in range(2)]


def exchange(value, axis, flip, size):
    return lax.ppermute(value, axis, [(i, i ^ flip) for i in range(size)])


def swap_if(flag, first, second):
    return jnp.where(flag, second, first), jnp.where(flag, first, second)


def together(*values):
    return lax.optimization_barrier(values)


def tokens_of_core(tokens):
    core = lax.axis_index("core")
    half = tokens.shape[1] // 2
    mine, other = swap_if(core == 1, tokens[:, :half], tokens[:, half:])
    return jnp.concatenate(swap_if(core == 1, mine, exchange(other, "core", 1, 2)), axis=1)


def tokens_of_pair(near):
    half = near.shape[1] // 2
    far = exchange(near, "xl", 1, 2)
    return jnp.concatenate([near[:, :half], far[:, :half], near[:, half:], far[:, half:]], axis=1)


def along_y(value, shift):
    return lax.ppermute(value, "y", [(i, (i + shift) % 4) for i in range(4)])


def gather_along_y(both):
    up, down = along_y(both, 1), along_y(both, -1)
    return [both, up, down, along_y(up[0], 1), along_y(down[1], -1)]


def order_blocks(place, here, up, down, far_up, far_down, out):
    width = out.shape[2]
    at = lax.rem(place[0] + 8 - pl.program_id(0), 8)
    columns = pl.ds(pl.multiple_of(lax.rem(at, 2) * width, width), width)
    shift = lax.rem(lax.div(at, 2) + 4 - place[1], 4)
    for s, piece in ((0, here), (3, up), (1, down)):

        @pl.when(shift == s)
        def copy():
            for e in range(2):
                out[e] = piece[e, :, columns]

    @pl.when(shift == 2)
    def copy_far():
        out[0] = far_up[:, columns]
        out[1] = far_down[:, columns]


def order_tokens(pieces):
    two, rows, columns = pieces[0].shape
    place = jnp.stack([lax.axis_index("z"), lax.axis_index("y")])
    ordered = pl.pallas_call(
        order_blocks,
        grid=(8,),
        in_specs=[pl.BlockSpec(memory_space=pltpu.SMEM)]
        + [pl.BlockSpec(piece.shape, lambda r, n=piece.ndim: (0,) * n) for piece in pieces],
        out_specs=pl.BlockSpec((two, rows, columns // 2), lambda r: (0, 0, r)),
        out_shape=jax.ShapeDtypeStruct((two, rows, 4 * columns), pieces[0].dtype),
        compiler_params=pltpu.CompilerParams(vmem_limit_bytes=40 * 2**20),
        cost_estimate=pl.CostEstimate(
            flops=0, transcendentals=0, bytes_accessed=16 * two * rows * columns
        ),
    )(place, *pieces)
    return ordered.reshape(two * rows, 4 * columns)


def along_z(value, shift):
    return lax.ppermute(value, "z", [(i, (i + shift) % 8) for i in range(8)])


def step_along_z(up, down):
    return along_z(up, 1), along_z(down, -1)


def product(gathered, blocks, half):
    total = 0
    for block, piece in blocks:
        features = gathered[:, block * half : block * half + piece.shape[0]]
        total += jnp.dot(features, piece, preferred_element_type=jnp.float32)
    return total


def swapped(weight):
    xh, xl, core = (lax.axis_index(name) for name in ("xh", "xl", "core"))
    half = weight.shape[0] // 2
    first, second = swap_if(xh == 1, weight[:half], weight[half:])
    turned = lax.ppermute(first, ("xh", "core"), TURN)
    crossed = lax.ppermute(second, ("xh", "core"), CROSS)
    return jnp.concatenate(swap_if(xl != core, turned, crossed))


def activate(total):
    rows = total.shape[0] // 2
    core = lax.axis_index("core")
    kept, given = swap_if(core == 1, total[:rows], total[rows:])
    total = kept + exchange(given, "core", 1, 2)
    return jax.nn.silu(total).astype(jnp.bfloat16)


def home(out):
    return lax.ppermute(out, ("xh", "core"), HOME)


def on_device(tokens, weight):
    half = weight.shape[0] // 2
    mine, tokens = together(swapped(weight[:, :FIRST]), tokens)
    up, down = together(*step_along_z(mine, mine))
    near, rest = together(tokens_of_core(tokens), weight[:, FIRST:])
    rest = swapped(rest)
    rest_up, rest_down = together(*step_along_z(rest, rest))
    piece, up, down = together(tokens_of_pair(near), up, down)
    beside = exchange(piece, "xh", 1, 2)
    both = jnp.stack([piece, beside])
    pieces = gather_along_y(both)
    mine = jnp.concatenate([mine, rest], axis=1)
    up = jnp.concatenate([up, rest_up], axis=1)
    down = jnp.concatenate([down, rest_down], axis=1)
    blocks = [(0, mine), (2, up), (14, down)]
    for step in range(2, 4):
        up, down = together(*step_along_z(up, down))
        if step == 2:
            tied_up, tied_down, *pieces = together(up, down, *pieces)
            blocks += [(2 * step, tied_up), (2 * (8 - step), tied_down)]
    gathered = order_tokens(pieces)
    early = product(gathered, blocks[:5], half)
    early, up, down = together(early, up, down)
    quarter = slice(0, half), slice(half, None)
    sent = [
        (up[quarter[0], columns], down[quarter[1], columns])
        for columns in (slice(0, LAST), slice(LAST, None))
    ]
    late_up, late_down, *sent[1] = together(up, down, *sent[1])
    ends = [step_along_z(*pair) for pair in sent]
    up, down = together(*ends[0])
    early += product(gathered, [(6, late_up), (10, late_down)], half)
    total = early[:, :LAST] + product(gathered, ((8, up), (9, down)), half)
    total, up, down = together(total, *ends[1])
    first = home(activate(total))
    second = activate(early[:, LAST:] + product(gathered, ((8, up), (9, down)), half))
    return jnp.concatenate([first, home(second)], axis=1)


def solution(mesh):
    fine = Mesh(mesh.devices.reshape(SIZES), AXES)
    placed = P(("xh", "z"), ("xl", "y", "core"))
    return jax.shard_map(
        on_device, mesh=fine, in_specs=(placed, placed), out_specs=placed, check_vma=False
    )
```

```python
import jax
import jax.numpy as jnp
from jax import lax
from jax.experimental import pallas as pl
from jax.experimental.pallas import tpu as pltpu
from jax.sharding import Mesh, PartitionSpec as P

AXES = ("xh", "z", "xl", "y", "core")
SIZES = (2, 8, 2, 4, 2)
FIRST = 896
LAST = 1024

TURN = [(h * 2 + c, c * 2 + h) for h in range(2) for c in range(2)]
CROSS = [(h * 2 + c, c * 2 + 1 - h) for h in range(2) for c in range(2)]
HOME = [(h * 2 + c, (h ^ c) * 2 + h) for h in range(2) for c in range(2)]


def exchange(value, axis, flip, size):
    return lax.ppermute(value, axis, [(i, i ^ flip) for i in range(size)])


def swap_if(flag, first, second):
    return jnp.where(flag, second, first), jnp.where(flag, first, second)


def together(*values):
    return lax.optimization_barrier(values)


def tokens_of_core(tokens):
    core = lax.axis_index("core")
    half = tokens.shape[1] // 2
    mine, other = swap_if(core == 1, tokens[:, :half], tokens[:, half:])
    return jnp.concatenate(swap_if(core == 1, mine, exchange(other, "core", 1, 2)), axis=1)


def tokens_of_pair(near):
    half = near.shape[1] // 2
    far = exchange(near, "xl", 1, 2)
    return jnp.concatenate([near[:, :half], far[:, :half], near[:, half:], far[:, half:]], axis=1)


def along_y(value, shift):
    return lax.ppermute(value, "y", [(i, (i + shift) % 4) for i in range(4)])


def gather_along_y(both):
    up, down = along_y(both, 1), along_y(both, -1)
    return [both, up, down, along_y(up[0], 1), along_y(down[1], -1)]


def order_blocks(place, here, up, down, far_up, far_down, out):
    width = out.shape[2]
    at = lax.rem(place[0] + 8 - pl.program_id(0), 8)
    columns = pl.ds(pl.multiple_of(lax.rem(at, 2) * width, width), width)
    shift = lax.rem(lax.div(at, 2) + 4 - place[1], 4)
    for s, piece in ((0, here), (3, up), (1, down)):

        @pl.when(shift == s)
        def copy():
            for e in range(2):
                out[e] = piece[e, :, columns]

    @pl.when(shift == 2)
    def copy_far():
        out[0] = far_up[:, columns]
        out[1] = far_down[:, columns]


def order_tokens(pieces):
    two, rows, columns = pieces[0].shape
    place = jnp.stack([lax.axis_index("z"), lax.axis_index("y")])
    ordered = pl.pallas_call(
        order_blocks,
        grid=(8,),
        in_specs=[pl.BlockSpec(memory_space=pltpu.SMEM)]
        + [pl.BlockSpec(piece.shape, lambda r, n=piece.ndim: (0,) * n) for piece in pieces],
        out_specs=pl.BlockSpec((two, rows, columns // 2), lambda r: (0, 0, r)),
        out_shape=jax.ShapeDtypeStruct((two, rows, 4 * columns), pieces[0].dtype),
        compiler_params=pltpu.CompilerParams(vmem_limit_bytes=40 * 2**20),
        cost_estimate=pl.CostEstimate(
            flops=0, transcendentals=0, bytes_accessed=16 * two * rows * columns
        ),
    )(place, *pieces)
    return ordered.reshape(two * rows, 4 * columns)


def along_z(value, shift):
    return lax.ppermute(value, "z", [(i, (i + shift) % 8) for i in range(8)])


def step_along_z(up, down):
    return along_z(up, 1), along_z(down, -1)


def product(gathered, blocks, half):
    total = 0
    for block, piece in blocks:
        features = gathered[:, block * half : block * half + piece.shape[0]]
        total += jnp.dot(features, piece, preferred_element_type=jnp.float32)
    return total


def swapped(weight):
    xh, xl, core = (lax.axis_index(name) for name in ("xh", "xl", "core"))
    half = weight.shape[0] // 2
    first, second = swap_if(xh == 1, weight[:half], weight[half:])
    turned = lax.ppermute(first, ("xh", "core"), TURN)
    crossed = lax.ppermute(second, ("xh", "core"), CROSS)
    return jnp.concatenate(swap_if(xl != core, turned, crossed))


def activate(total):
    rows = total.shape[0] // 2
    core = lax.axis_index("core")
    kept, given = swap_if(core == 1, total[:rows], total[rows:])
    total = kept + exchange(given, "core", 1, 2)
    return jax.nn.silu(total).astype(jnp.bfloat16)


def home(out):
    return lax.ppermute(out, ("xh", "core"), HOME)


def on_device(tokens, weight):
    half = weight.shape[0] // 2
    mine, tokens = together(swapped(weight[:, :FIRST]), tokens)
    up, down = together(*step_along_z(mine, mine))
    near, rest = together(tokens_of_core(tokens), weight[:, FIRST:])
    rest = swapped(rest)
    rest_up, rest_down = together(*step_along_z(rest, rest))
    piece, up, down = together(tokens_of_pair(near), up, down)
    beside = exchange(piece, "xh", 1, 2)
    both = jnp.stack([piece, beside])
    pieces = gather_along_y(both)
    mine = jnp.concatenate([mine, rest], axis=1)
    up = jnp.concatenate([up, rest_up], axis=1)
    down = jnp.concatenate([down, rest_down], axis=1)
    blocks = [(0, mine), (2, up), (14, down)]
    for step in range(2, 4):
        up, down = together(*step_along_z(up, down))
        if step == 2:
            tied_up, tied_down, *pieces = together(up, down, *pieces)
            blocks += [(2 * step, tied_up), (2 * (8 - step), tied_down)]
    gathered = order_tokens(pieces)
    early = product(gathered, blocks[:5], half)
    early, up, down = together(early, up, down)
    quarter = slice(0, half), slice(half, None)
    sent = [
        (up[quarter[0], columns], down[quarter[1], columns])
        for columns in (slice(0, LAST), slice(LAST, None))
    ]
    late_up, late_down, *sent[1] = together(up, down, *sent[1])
    ends = [step_along_z(*pair) for pair in sent]
    up, down = together(*ends[0])
    early += product(gathered, [(6, late_up), (10, late_down)], half)
    total = early[:, :LAST] + product(gathered, ((8, up), (9, down)), half)
    total, up, down = together(total, *ends[1])
    first = home(activate(total))
    second = activate(early[:, LAST:] + product(gathered, ((8, up), (9, down)), half))
    return jnp.concatenate([first, home(second)], axis=1)


def solution(mesh):
    fine = Mesh(mesh.devices.reshape(SIZES), AXES)
    placed = P(("xh", "z"), ("xl", "y", "core"))
    return jax.shard_map(
        on_device, mesh=fine, in_specs=(placed, placed), out_specs=placed, check_vma=False
    )
```
